512 devices in a mesh: row: 16 (over y, core), col: 32 (over z, x).
Axes of the slice: x: 4, y: 8, z: 8, core: 2. Of those that a mesh axis runs over, the one named last changes fastest.
Arguments:
- features: bfloat16 [65536, 128], P(('row', 'col')), may hold values from -6 to 6
- block_values: bfloat16 [16, 32, 128, 128, 128], P('row', 'col'), may hold values from -0.046875 to 0.046875
- block_rows: int32 [16, 32, 128], P('row', 'col'), may hold values from 0 to 31
- block_cols: int32 [16, 32, 128], P('row', 'col'), may hold values from 0 to 15
- counts: int32 [16, 32], P('row', 'col'), may hold values from 16 to 128, as said below
- weight: float32 [128, 128], replicated, may hold values from -0.5 to 0.5
- bias: float32 [128], replicated, may hold values from -3 to 3
- cotangent: bfloat16 [65536, 128], P(('row', 'col')), may hold values from -6 to 6
Outputs:
- hidden: float32 [65536, 128], P(('row', 'col'))
- grad_features: float32 [65536, 128], P(('row', 'col'))
- grad_weight: float32 [128, 128], replicated
- grad_bias: float32 [128], replicated
The draws below stay inside these ranges and needn't reach their ends.
Inputs may be any that keep to these rules, and one draw needn't show every extreme that they name: `counts`: some tile has all 128 slots live.
All inputs are finite; a program needn't handle non-finite values.
Results may differ from the reference program's by a relative error of at most 0.0029.
Values may be sent and summed in bfloat16 or wider, within the bound.
A program may use at most 128 MiB of HBM per device.

```python
import jax
import jax.numpy as jnp
from jax import lax

BS = 128
F = 128
H = 128
MAXB = 128
NODES = 65536
N_ROW = 16
N_COL = 32


def draw_counts(key, part):
    key_shift, key_reduce, key_chosen = jax.random.split(key, 3)
    tile_shape = (N_ROW, N_COL)
    shift_amount = jax.random.randint(key_shift, tile_shape, 0, 3)
    base_count = jnp.where(shift_amount == 0, MAXB, jnp.where(shift_amount == 1, MAXB // 2, MAXB // 4)).astype(jnp.int32)
    reduction = jax.random.randint(key_reduce, tile_shape, 0, base_count // 2 + 1)
    drawn = (base_count - reduction).reshape(-1)
    chosen = jax.random.randint(key_chosen, (), 0, N_ROW * N_COL)
    flattened = jnp.where(jnp.arange(N_ROW * N_COL) == chosen, MAXB, drawn)
    return flattened.reshape(tile_shape).astype(jnp.int32)


def plant(array, own_key, low, largest):
    shape = array.shape
    place = [jax.random.randint(jax.random.fold_in(own_key, axis), (), 0, shape[axis]) for axis in range(len(shape))]
    array = array.at[tuple(place)].set(low)
    longest = shape.index(max(shape))
    place[longest] = (place[longest] + 1) % shape[longest]
    return array.at[tuple(place)].set(largest)


def block_scale(stream_key, dims, shards, least, largest):
    def one(position, parts):
        steps = jax.random.uniform(jax.random.fold_in(jax.random.fold_in(stream_key, 6), position), (parts,), jnp.float32, least / len(shards), largest / len(shards))
        return jnp.repeat(jnp.exp(steps), dims[position] // parts).reshape((-1,) + (1,) * (len(dims) - position - 1))

    level = one(*shards[0])
    for cut in shards[1:]:
        level = level * one(*cut)
    return level


def normal_values(rng, dims, width, limit, cuts=(), held_as=jnp.bfloat16):
    values = jax.random.normal(rng, dims, jnp.float32) * width
    if len(cuts) > 0:
        values = block_scale(rng, dims, cuts, -0.22, 0.18) * values
    return jnp.clip(values, min=-limit, max=limit).astype(held_as)


def setup_inputs(seed: int = 0) -> dict:
    arg_keys = jax.random.split(jax.random.key(seed), 9)
    features = normal_values(arg_keys[0], (NODES, F), 1.0, 6.0, ((0, 512),))
    block_values = normal_values(arg_keys[1], (N_ROW, N_COL, MAXB, BS, BS), (MAXB * BS) ** -0.5, 0.046875, ((0, 16), (1, 32)))
    block_rows = plant(jax.random.randint(arg_keys[2], (N_ROW, N_COL, MAXB), 0, N_COL), jax.random.fold_in(arg_keys[2], 1), 0, N_COL - 1).astype(jnp.int32)
    block_cols = plant(jax.random.randint(arg_keys[3], (N_ROW, N_COL, MAXB), 0, N_ROW), jax.random.fold_in(arg_keys[3], 1), 0, N_ROW - 1).astype(jnp.int32)
    counts = draw_counts(jax.random.fold_in(arg_keys[8], 71), 0)
    weight = normal_values(arg_keys[5], (F, H), F ** -0.5, 0.5, (), jnp.float32)
    bias = normal_values(arg_keys[6], (H,), 0.5, 3.0, (), jnp.float32)
    cotangent = normal_values(arg_keys[7], (NODES, H), 1.0, 6.0, ((0, 512),))
    return {"features": features, "block_values": block_values, "block_rows": block_rows, "block_cols": block_cols, "counts": counts, "weight": weight, "bias": bias, "cotangent": cotangent}


def reference(features, block_values, block_rows, block_cols, counts, weight, bias, cotangent):
    feature_blocks = features.astype(jnp.float32).reshape(N_ROW, N_COL, BS, F)
    slot_ids = jnp.arange(MAXB).astype(jnp.int32)

    def tile_forward(tile_row, tile_col):
        tile_values = block_values[tile_row, tile_col].astype(jnp.float32)
        source = feature_blocks[:, tile_col]
        picked = source[block_cols[tile_row, tile_col].astype(jnp.int32)]
        products = jnp.einsum('kab,kbf->kaf', tile_values, picked, precision=lax.Precision.HIGHEST)
        live_mask = (slot_ids < counts[tile_row, tile_col]).astype(jnp.float32)
        onehot = (block_rows[tile_row, tile_col][None, :] == jnp.arange(N_COL).astype(jnp.int32)[:, None]).astype(jnp.float32) * live_mask[None, :]
        return jnp.einsum('ak,kbf->abf', onehot, products, precision=lax.Precision.HIGHEST)

    def row_total(tile_row):

        def accumulate(totals, tile_col):
            return (totals + tile_forward(tile_row, tile_col), None)
        totals, _ = lax.scan(accumulate, jnp.zeros((N_COL, BS, F), jnp.float32), jnp.arange(N_COL).astype(jnp.int32))
        return totals
    aggregated = lax.map(row_total, jnp.arange(N_ROW).astype(jnp.int32)).reshape(NODES, F)
    pre_act = jnp.dot(aggregated, weight, precision=lax.Precision.HIGHEST) + bias[None, :]
    sigm = 1.0 / (1.0 + jnp.exp(-pre_act))
    hidden = pre_act * sigm
    masked_grad = cotangent.astype(jnp.float32) * sigm * (1.0 + pre_act * (1.0 - sigm))
    grad_rows = jnp.dot(masked_grad, weight.T, precision=lax.Precision.HIGHEST).astype(jnp.bfloat16)
    grad_blocks = grad_rows.astype(jnp.float32).reshape(N_ROW, N_COL, BS, F)

    def tile_backward(tile_row, tile_col):
        tile_values = block_values[tile_row, tile_col].astype(jnp.float32)
        picked = grad_blocks[tile_row][block_rows[tile_row, tile_col].astype(jnp.int32)]
        products = jnp.einsum('kab,kaf->kbf', tile_values, picked, precision=lax.Precision.HIGHEST)
        live_mask = (slot_ids < counts[tile_row, tile_col]).astype(jnp.float32)
        onehot = (block_cols[tile_row, tile_col][None, :] == jnp.arange(N_ROW).astype(jnp.int32)[:, None]).astype(jnp.float32) * live_mask[None, :]
        return jnp.einsum('ak,kbf->abf', onehot, products, precision=lax.Precision.HIGHEST)

    def col_total(tile_col):

        def accumulate(totals, tile_row):
            return (totals + tile_backward(tile_row, tile_col), None)
        totals, _ = lax.scan(accumulate, jnp.zeros((N_ROW, BS, F), jnp.float32), jnp.arange(N_ROW).astype(jnp.int32))
        return totals
    column_sums = lax.map(col_total, jnp.arange(N_COL).astype(jnp.int32))
    grad_features = jnp.transpose(column_sums, (1, 0, 2, 3)).reshape(NODES, F)
    norm_factor = 1.0 / jnp.sqrt(jnp.float32(NODES))
    grad_weight = jnp.dot(aggregated.T, masked_grad, precision=lax.Precision.HIGHEST) * norm_factor
    grad_bias = lax.optimization_barrier(jnp.sum(masked_grad, axis=0)) * norm_factor
    return (hidden, grad_features, grad_weight, grad_bias)
```

```python
import functools
import math

import jax
import jax.numpy as jnp
from jax import lax
from jax.experimental import pallas as pl
from jax.experimental.pallas import tpu as pltpu
from jax.sharding import PartitionSpec as P

MESH = pl.DeviceIdType.MESH
CHUNK = 16


def product_kernel(transposed, out_blocks, dest_ref, from_ref, count_ref, values_ref, source_ref, out_ref, totals):
    step = pl.program_id(0)
    live = count_ref[0]

    @pl.when(step == 0)
    def _():
        totals[...] = jnp.zeros_like(totals)

    @pl.when(step * CHUNK < live)
    def _():
        for k in range(CHUNK):
            slot = step * CHUNK + k
            dest = jnp.where(slot < live, dest_ref[slot], out_blocks)
            block = values_ref[k]
            source = source_ref[from_ref[slot]]
            if transposed:
                part = jnp.dot(source, block, preferred_element_type=jnp.float32)
            else:
                part = jnp.dot(block, source, preferred_element_type=jnp.float32)
            totals[dest] += part

    @pl.when(step == pl.num_programs(0) - 1)
    def _():
        out_ref[...] = totals[0:out_blocks].astype(out_ref.dtype)


def tile_product(values, dest, source_of, count, source, out_blocks, transposed, out_dtype):
    slots, size, _ = values.shape
    width = source.shape[2]
    return pl.pallas_call(
        functools.partial(product_kernel, transposed, out_blocks),
        grid_spec=pltpu.PrefetchScalarGridSpec(
            num_scalar_prefetch=3,
            grid=(slots // CHUNK,),
            in_specs=[
                pl.BlockSpec((CHUNK, size, size), lambda i, *_: (i, 0, 0)),
                pl.BlockSpec(source.shape, lambda i, *_: (0, 0, 0)),
            ],
            out_specs=pl.BlockSpec((out_blocks, size, width), lambda i, *_: (0, 0, 0)),
            scratch_shapes=[pltpu.VMEM((out_blocks + 1, size, width), jnp.float32)],
        ),
        out_shape=jax.ShapeDtypeStruct((out_blocks, size, width), out_dtype),
        compiler_params=pltpu.CompilerParams(dimension_semantics=("arbitrary",)),
    )(dest, source_of, count, values, source)


def exchange_kernel(axis, n, kinds, *refs):
    m = len(kinds)
    sources, outs, held = refs[:m], refs[m : 2 * m], refs[2 * m : 3 * m]
    send_sem, recv_sem = refs[3 * m], refs[3 * m + 1]
    me = lax.axis_index(axis)
    row, col = lax.axis_index("row"), lax.axis_index("col")

    def device(peer):
        return (row, peer) if axis == "col" else (peer, col)

    def partner(k):
        half = k // 2 + 1
        return lax.rem(me + jnp.where(k % 2 == 0, half, n - half), n)

    def copy(i, to, slot):
        source = sources[i].at[to] if kinds[i] == "scatter" else sources[i]
        return pltpu.make_async_remote_copy(
            src_ref=source,
            dst_ref=held[i].at[slot],
            send_sem=send_sem.at[i, to],
            recv_sem=recv_sem.at[i, slot],
            device_id=device(to),
            device_id_type=MESH,
        )

    barrier = pltpu.get_barrier_semaphore()

    @pl.loop(0, n - 1)
    def _(k):
        pl.semaphore_signal(barrier, inc=1, device_id=device(partner(k)), device_id_type=MESH)

    pl.semaphore_wait(barrier, n - 1)

    @pl.loop(0, n - 1)
    def _(k):
        for i in range(m):
            copy(i, partner(k), me).start()

    for i in range(m):
        held[i][me] = sources[i][me] if kinds[i] == "scatter" else sources[i][...]

    @pl.loop(0, n - 1)
    def _(k):
        for i in range(m):
            copy(i, partner(k), partner(k)).wait_recv()

    for i in range(m):
        if kinds[i] == "gather":
            outs[i][...] = held[i][...]
        else:

            def add(s, total):
                return total + held[i][s].astype(jnp.float32)

            outs[i][...] = lax.fori_loop(0, n, add, jnp.zeros(outs[i].shape, jnp.float32))

    @pl.loop(0, n - 1)
    def _(k):
        for i in range(m):
            copy(i, partner(k), partner(k)).wait_send()


def exchange(axis, number, *items):
    n = lax.axis_size(axis)
    kinds = tuple(kind for kind, _ in items)
    arrays = [array for _, array in items]
    blocks = [a.shape[1:] if kind == "scatter" else a.shape for kind, a in items]
    vmem = pl.BlockSpec(memory_space=pltpu.VMEM)
    return pl.pallas_call(
        functools.partial(exchange_kernel, axis, n, kinds),
        out_shape=[
            jax.ShapeDtypeStruct((n,) + block, a.dtype) if kind == "gather" else jax.ShapeDtypeStruct(block, jnp.float32)
            for (kind, a), block in zip(items, blocks)
        ],
        in_specs=[vmem] * len(items),
        out_specs=[vmem] * len(items),
        scratch_shapes=[pltpu.VMEM((n,) + block, a.dtype) for a, block in zip(arrays, blocks)]
        + [pltpu.SemaphoreType.DMA((len(items), n)), pltpu.SemaphoreType.DMA((len(items), n))],
        compiler_params=pltpu.CompilerParams(collective_id=number, has_side_effects=True),
    )(*arrays)


def per_device(features, block_values, block_rows, block_cols, counts, weight, bias, cotangent):
    size, width = features.shape
    hidden_width = weight.shape[1]
    row_count = lax.axis_size("row")
    col_count = lax.axis_size("col")
    values = block_values[0, 0]
    rows = block_rows[0, 0]
    cols = block_cols[0, 0]
    count = counts[0]

    (column_feats,) = exchange("row", 0, ("gather", features))
    partial = tile_product(values, rows, cols, count, column_feats, col_count, False, jnp.bfloat16)
    (aggregated,) = exchange("col", 1, ("scatter", partial))

    highest = lax.Precision.HIGHEST
    pre_act = jnp.dot(aggregated, weight, precision=highest) + bias[None, :]
    sigm = 1.0 / (1.0 + jnp.exp(-pre_act))
    hidden = pre_act * sigm
    masked_grad = cotangent.astype(jnp.float32) * sigm * (1.0 + pre_act * (1.0 - sigm))
    grad_own = lax.dot_general(
        weight, masked_grad, (((1,), (1,)), ((), ())), precision=highest
    ).astype(jnp.bfloat16)
    norm_factor = 1.0 / math.sqrt(size * row_count * col_count)
    weight_part = jnp.dot(aggregated.T, masked_grad, precision=highest) * norm_factor
    bias_part = jnp.sum(masked_grad, axis=0) * norm_factor
    per_slice = width // col_count
    slices = jnp.concatenate(
        [
            weight_part.reshape(col_count, per_slice, hidden_width),
            jnp.broadcast_to(bias_part, (col_count, 1, hidden_width)),
            jnp.zeros((col_count, -(per_slice + 1) % 8, hidden_width), jnp.float32),
        ],
        axis=1,
    )

    grad_row, col_slice = exchange("col", 2, ("gather", grad_own), ("scatter", slices))
    back = tile_product(values, cols, rows, count, grad_row, row_count, True, jnp.bfloat16)
    grad_t, own_slice = exchange("row", 3, ("scatter", back), ("collect", col_slice))
    (all_slices,) = exchange("col", 4, ("gather", own_slice))
    grad_weight = all_slices[:, :per_slice].reshape(width, hidden_width)
    grad_bias = all_slices[0, per_slice]
    return (hidden, grad_t.T, grad_weight, grad_bias)


def solution(mesh):
    placed = (
        P(("row", "col"), None),
        P("row", "col", None, None, None),
        P("row", "col", None),
        P("row", "col", None),
        P("row", "col"),
        P(),
        P(),
        P(("row", "col"), None),
    )
    return jax.shard_map(
        per_device,
        mesh=mesh,
        in_specs=placed,
        out_specs=(P(("row", "col"), None), P(("row", "col"), None), P(), P()),
        check_vma=False,
    )
```

```python
import functools
import math

import jax
import jax.numpy as jnp
from jax import lax
from jax.experimental import pallas as pl
from jax.experimental.pallas import tpu as pltpu
from jax.sharding import PartitionSpec as P

MESH = pl.DeviceIdType.MESH
CHUNK = 16
INNER = {"row": 2, "col": 4}


def product_kernel(transposed, out_blocks, dest_ref, from_ref, count_ref, values_ref, source_ref, out_ref, totals):
    step = pl.program_id(0)
    live = count_ref[0]

    @pl.when(step == 0)
    def _():
        totals[...] = jnp.zeros_like(totals)

    @pl.when(step * CHUNK < live)
    def _():
        for k in range(CHUNK):
            slot = step * CHUNK + k
            dest = jnp.where(slot < live, dest_ref[slot], out_blocks)
            block = values_ref[k]
            source = source_ref[from_ref[slot]]
            if transposed:
                part = jnp.dot(source, block, preferred_element_type=jnp.float32)
            else:
                part = jnp.dot(block, source, preferred_element_type=jnp.float32)
            totals[dest] += part

    @pl.when(step == pl.num_programs(0) - 1)
    def _():
        out_ref[...] = totals[0:out_blocks].astype(out_ref.dtype)


def tile_product(values, dest, source_of, count, source, out_blocks, transposed, out_dtype):
    slots, size, _ = values.shape
    width = source.shape[2]
    return pl.pallas_call(
        functools.partial(product_kernel, transposed, out_blocks),
        grid_spec=pltpu.PrefetchScalarGridSpec(
            num_scalar_prefetch=3,
            grid=(slots // CHUNK,),
            in_specs=[
                pl.BlockSpec((CHUNK, size, size), lambda i, *_: (i, 0, 0)),
                pl.BlockSpec(source.shape, lambda i, *_: (0, 0, 0)),
            ],
            out_specs=pl.BlockSpec((out_blocks, size, width), lambda i, *_: (0, 0, 0)),
            scratch_shapes=[pltpu.VMEM((out_blocks + 1, size, width), jnp.float32)],
        ),
        out_shape=jax.ShapeDtypeStruct((out_blocks, size, width), out_dtype),
        compiler_params=pltpu.CompilerParams(dimension_semantics=("arbitrary",)),
    )(dest, source_of, count, values, source)


class Group:
    def __init__(self, axis):
        self.axis = axis
        self.n = lax.axis_size(axis)
        self.inner = INNER[axis]
        self.outer = self.n // self.inner
        self.me = lax.axis_index(axis)
        self.o = self.me // self.inner
        self.i = lax.rem(self.me, self.inner)
        self.row, self.col = lax.axis_index("row"), lax.axis_index("col")

    def device(self, peer):
        return (self.row, peer) if self.axis == "col" else (peer, self.col)

    def others_outer(self, k):
        half = k // 2 + 1
        return lax.rem(self.o + jnp.where(k % 2 == 0, half, self.outer - half), self.outer)

    def others_inner(self):
        return [lax.rem(self.i + d, self.inner) for d in range(1, self.inner)]

    def partner(self, k):
        half = k // 2 + 1
        return lax.rem(self.me + jnp.where(k % 2 == 0, half, self.n - half), self.n)

    def copy(self, src, dst, send, recv, peer):
        return pltpu.make_async_remote_copy(
            src_ref=src, dst_ref=dst, send_sem=send, recv_sem=recv,
            device_id=self.device(peer), device_id_type=MESH,
        )

    def hello(self, every):
        barrier = pltpu.get_barrier_semaphore()

        def greet(peer):
            pl.semaphore_signal(barrier, inc=1, device_id=self.device(peer), device_id_type=MESH)

        if every:

            @pl.loop(0, self.n - 1)
            def _(k):
                greet(self.partner(k))

            return self.n - 1

        @pl.loop(0, self.outer - 1)
        def _(k):
            greet(self.others_outer(k) * self.inner + self.i)

        for i in self.others_inner():
            greet(self.o * self.inner + i)
        return self.outer - 1 + self.inner - 1


class Gather:
    def __init__(self, group, src, held, send, recv):
        self.g, self.src, self.held, self.send, self.recv = group, src, held, send, recv

    def to_outer(self, o):
        g = self.g
        peer = o * g.inner + g.i
        return g.copy(self.src, self.held.at[g.me], self.send.at[peer], self.recv.at[g.me], peer)

    def from_slot(self, slot, peer):
        return self.g.copy(self.src, self.held.at[slot], self.send.at[slot], self.recv.at[slot], peer)

    def forward(self, o, i):
        g = self.g
        slot = o * g.inner + g.i
        return g.copy(self.held.at[slot], self.held.at[slot], self.send.at[o * g.inner + i],
                      self.recv.at[slot], g.o * g.inner + i)

    def own_inner(self, i):
        g = self.g
        peer = g.o * g.inner + i
        return g.copy(self.src, self.held.at[g.me], self.send.at[peer], self.recv.at[g.me], peer)

    def start(self):
        g = self.g

        @pl.loop(0, g.outer - 1)
        def _(k):
            self.to_outer(g.others_outer(k)).start()

        for i in g.others_inner():
            self.own_inner(i).start()

    def relay(self):
        g = self.g

        @pl.loop(0, g.outer - 1)
        def _(k):
            o = g.others_outer(k)
            slot = o * g.inner + g.i
            self.from_slot(slot, slot).wait_recv()
            for i in g.others_inner():
                self.forward(o, i).start()

    def finish(self):
        g = self.g
        for i in g.others_inner():
            peer = g.o * g.inner + i
            self.from_slot(peer, peer).wait_recv()

        @pl.loop(0, g.outer - 1)
        def _(k):
            o = g.others_outer(k)
            for i in g.others_inner():
                slot = o * g.inner + i
                self.from_slot(slot, g.o * g.inner + i).wait_recv()

    def drain(self):
        g = self.g

        @pl.loop(0, g.outer - 1)
        def _(k):
            o = g.others_outer(k)
            self.to_outer(o).wait_send()
            for i in g.others_inner():
                self.forward(o, i).wait_send()

        for i in g.others_inner():
            self.own_inner(i).wait_send()


class Scatter:
    def __init__(self, group, src, near, sums, far, send1, recv1, send2, recv2):
        self.g, self.src, self.near, self.sums, self.far = group, src, near, sums, far
        self.send1, self.recv1, self.send2, self.recv2 = send1, recv1, send2, recv2

    def along_inner(self, o, i):
        g = self.g
        slot = o * g.inner + i
        return g.copy(self.src.at[slot], self.near.at[o * g.inner + g.i], self.send1.at[slot],
                      self.recv1.at[o * g.inner + g.i], g.o * g.inner + i)

    def arrived_inner(self, o, i):
        g = self.g
        slot = o * g.inner + i
        return g.copy(self.src.at[slot], self.near.at[slot], self.send1.at[slot], self.recv1.at[slot],
                      g.o * g.inner + i)

    def along_outer(self, o):
        g = self.g
        return g.copy(self.sums.at[o], self.far.at[g.o], self.send2.at[o], self.recv2.at[g.o], o * g.inner + g.i)

    def arrived_outer(self, o):
        g = self.g
        return g.copy(self.sums.at[o], self.far.at[o], self.send2.at[o], self.recv2.at[o], o * g.inner + g.i)

    def start(self):
        g = self.g

        @pl.loop(0, g.outer - 1)
        def _(k):
            for i in g.others_inner():
                self.along_inner(g.others_outer(k), i).start()

        for i in g.others_inner():
            self.along_inner(g.o, i).start()

    def near_sum(self, o):
        g = self.g
        for i in g.others_inner():
            self.arrived_inner(o, i).wait_recv()
        total = self.src[o * g.inner + g.i].astype(jnp.float32)
        for i in g.others_inner():
            total += self.near[o * g.inner + i].astype(jnp.float32)
        return total

    def relay(self):
        g = self.g

        @pl.loop(0, g.outer - 1)
        def _(k):
            o = g.others_outer(k)
            self.sums[o] = self.near_sum(o)
            self.along_outer(o).start()

    def finish(self):
        g = self.g
        own = self.near_sum(g.o)

        def add(k, total):
            o = g.others_outer(k)
            self.arrived_outer(o).wait_recv()
            return total + self.far[o]

        return lax.fori_loop(0, g.outer - 1, add, own)

    def drain(self):
        g = self.g

        @pl.loop(0, g.outer - 1)
        def _(k):
            o = g.others_outer(k)
            self.along_outer(o).wait_send()
            for i in g.others_inner():
                self.along_inner(o, i).wait_send()

        for i in g.others_inner():
            self.along_inner(g.o, i).wait_send()


def gather_kernel(axis, src, out, held, send, recv):
    g = Group(axis)
    gather = Gather(g, src, held, send, recv)
    pl.semaphore_wait(pltpu.get_barrier_semaphore(), g.hello(False))
    gather.start()
    held[g.me] = src[...]
    gather.relay()
    gather.finish()
    out[...] = held[...]
    gather.drain()


def scatter_kernel(axis, src, out, near, sums, far, send1, recv1, send2, recv2):
    g = Group(axis)
    scatter = Scatter(g, src, near, sums, far, send1, recv1, send2, recv2)
    pl.semaphore_wait(pltpu.get_barrier_semaphore(), g.hello(False))
    scatter.start()
    scatter.relay()
    out[...] = scatter.finish()
    scatter.drain()


def middle_kernel(src, slices, out, slice_out, held, send, recv, near, sums, far, send1, recv1, send2, recv2):
    g = Group("col")
    gather = Gather(g, src, held, send, recv)
    scatter = Scatter(g, slices, near, sums, far, send1, recv1, send2, recv2)
    pl.semaphore_wait(pltpu.get_barrier_semaphore(), g.hello(False))
    gather.start()
    scatter.start()
    held[g.me] = src[...]
    gather.relay()
    scatter.relay()
    slice_out[...] = scatter.finish()
    gather.finish()
    out[...] = held[...]
    gather.drain()
    scatter.drain()


def last_kernel(back, part, out, all_out, held, held_part, own, held_all, sb, rb, sp, rp, sa, ra):
    g, c = Group("row"), Group("col")
    gather = Gather(c, own, held_all, sa, ra)

    def block(peer, slot):
        return g.copy(back.at[peer], held.at[slot], sb.at[peer], rb.at[slot], peer)

    def piece(peer, slot):
        return g.copy(part, held_part.at[slot], sp.at[peer], rp.at[slot], peer)

    pl.semaphore_wait(pltpu.get_barrier_semaphore(), g.hello(True) + c.hello(False))

    @pl.loop(0, g.n - 1)
    def _(k):
        piece(g.partner(k), g.me).start()

    @pl.loop(0, g.n - 1)
    def _(k):
        block(g.partner(k), g.me).start()

    held_part[g.me] = part[...]

    @pl.loop(0, g.n - 1)
    def _(k):
        piece(g.partner(k), g.partner(k)).wait_recv()

    total = held_part[0]
    for s in range(1, g.n):
        total += held_part[s]
    own[...] = total
    held_all[c.me] = total
    gather.start()

    def add(k, total):
        block(g.partner(k), g.partner(k)).wait_recv()
        return total + held[g.partner(k)].astype(jnp.float32)

    gather.relay()
    out[...] = lax.fori_loop(0, g.n - 1, add, back[g.me].astype(jnp.float32))
    gather.finish()
    all_out[...] = held_all[...]
    gather.drain()

    @pl.loop(0, g.n - 1)
    def _(k):
        block(g.partner(k), g.partner(k)).wait_send()
        piece(g.partner(k), g.partner(k)).wait_send()


def call(kernel, number, outs, scratch, *arrays):
    vmem = pl.BlockSpec(memory_space=pltpu.VMEM)
    return pl.pallas_call(
        kernel,
        out_shape=outs,
        in_specs=[vmem] * len(arrays),
        out_specs=[vmem] * len(outs),
        scratch_shapes=scratch,
        compiler_params=pltpu.CompilerParams(collective_id=number, has_side_effects=True),
    )(*arrays)


def copies(*sizes):
    return [pltpu.SemaphoreType.DMA((size,)) for size in sizes]


def gather_scratch(n, block, dtype):
    return [pltpu.VMEM((n,) + block, dtype)] + copies(n, n)


def scatter_scratch(axis, block, dtype):
    n = lax.axis_size(axis)
    outer = n // INNER[axis]
    return [
        pltpu.VMEM((n,) + block, dtype),
        pltpu.VMEM((outer,) + block, jnp.float32),
        pltpu.VMEM((outer,) + block, jnp.float32),
    ] + copies(n, n, outer, outer)


def per_device(features, block_values, block_rows, block_cols, counts, weight, bias, cotangent):
    size, width = features.shape
    hidden_width = weight.shape[1]
    row_count = lax.axis_size("row")
    col_count = lax.axis_size("col")
    values = block_values[0, 0]
    rows = block_rows[0, 0]
    cols = block_cols[0, 0]
    count = counts[0]

    shape = jax.ShapeDtypeStruct
    block = (size, width)
    (column_feats,) = call(
        functools.partial(gather_kernel, "row"), 0, [shape((row_count,) + block, features.dtype)],
        gather_scratch(row_count, block, features.dtype), features,
    )
    partial = tile_product(values, rows, cols, count, column_feats, col_count, False, jnp.bfloat16)
    (aggregated,) = call(
        functools.partial(scatter_kernel, "col"), 1, [shape(block, jnp.float32)],
        scatter_scratch("col", block, partial.dtype), partial,
    )

    highest = lax.Precision.HIGHEST
    pre_act = jnp.dot(aggregated, weight, precision=highest) + bias[None, :]
    sigm = 1.0 / (1.0 + jnp.exp(-pre_act))
    hidden = pre_act * sigm
    masked_grad = cotangent.astype(jnp.float32) * sigm * (1.0 + pre_act * (1.0 - sigm))
    grad_own = lax.dot_general(
        weight, masked_grad, (((1,), (1,)), ((), ())), precision=highest
    ).astype(jnp.bfloat16)
    norm_factor = 1.0 / math.sqrt(size * row_count * col_count)
    weight_part = jnp.dot(aggregated.T, masked_grad, precision=highest) * norm_factor
    bias_part = jnp.sum(masked_grad, axis=0) * norm_factor
    per_slice = width // col_count
    slices = jnp.concatenate(
        [
            weight_part.reshape(col_count, per_slice, hidden_width),
            jnp.broadcast_to(bias_part, (col_count, 1, hidden_width)),
            jnp.zeros((col_count, -(per_slice + 1) % 8, hidden_width), jnp.float32),
        ],
        axis=1,
    )

    piece = slices.shape[1:]
    grad_row, col_slice = call(
        middle_kernel, 2, [shape((col_count,) + grad_own.shape, grad_own.dtype), shape(piece, jnp.float32)],
        gather_scratch(col_count, grad_own.shape, grad_own.dtype) + scatter_scratch("col", piece, jnp.float32),
        grad_own, slices,
    )
    back = tile_product(values, cols, rows, count, grad_row, row_count, True, jnp.bfloat16)
    grad_t, all_slices = call(
        last_kernel, 3, [shape(back.shape[1:], jnp.float32), shape((col_count,) + piece, jnp.float32)],
        [
            pltpu.VMEM(back.shape, back.dtype),
            pltpu.VMEM((row_count,) + piece, jnp.float32),
            pltpu.VMEM(piece, jnp.float32),
            pltpu.VMEM((col_count,) + piece, jnp.float32),
        ]
        + copies(row_count, row_count, row_count, row_count, col_count, col_count),
        back, col_slice,
    )
    grad_weight = all_slices[:, :per_slice].reshape(width, hidden_width)
    grad_bias = all_slices[0, per_slice]
    return (hidden, grad_t.T, grad_weight, grad_bias)


def solution(mesh):
    placed = (
        P(("row", "col"), None),
        P("row", "col", None, None, None),
        P("row", "col", None),
        P("row", "col", None),
        P("row", "col"),
        P(),
        P(),
        P(("row", "col"), None),
    )
    return jax.shard_map(
        per_device,
        mesh=mesh,
        in_specs=placed,
        out_specs=(P(("row", "col"), None), P(("row", "col"), None), P(), P()),
        check_vma=False,
    )
```

```python
import functools
import math

import jax
import jax.numpy as jnp
from jax import lax
from jax.experimental import pallas as pl
from jax.experimental.pallas import tpu as pltpu
from jax.sharding import PartitionSpec as P

MESH = pl.DeviceIdType.MESH
CHUNK = 16
INNER = {"row": 2, "col": 4}


def product_kernel(transposed, out_blocks, dest_ref, from_ref, count_ref, values_ref, source_ref, out_ref, totals):
    step = pl.program_id(0)
    live = count_ref[0]

    @pl.when(step == 0)
    def _():
        totals[...] = jnp.zeros_like(totals)

    @pl.when(step * CHUNK < live)
    def _():
        for k in range(CHUNK):
            slot = step * CHUNK + k
            dest = jnp.where(slot < live, dest_ref[slot], out_blocks)
            block = values_ref[k]
            source = source_ref[from_ref[slot]]
            if transposed:
                part = jnp.dot(source, block, preferred_element_type=jnp.float32)
            else:
                part = jnp.dot(block, source, preferred_element_type=jnp.float32)
            totals[dest] += part

    @pl.when(step == pl.num_programs(0) - 1)
    def _():
        out_ref[...] = totals[0:out_blocks].astype(out_ref.dtype)


def tile_product(values, dest, source_of, count, source, out_blocks, transposed, out_dtype):
    slots, size, _ = values.shape
    width = source.shape[2]
    return pl.pallas_call(
        functools.partial(product_kernel, transposed, out_blocks),
        grid_spec=pltpu.PrefetchScalarGridSpec(
            num_scalar_prefetch=3,
            grid=(slots // CHUNK,),
            in_specs=[
                pl.BlockSpec((CHUNK, size, size), lambda i, *_: (i, 0, 0)),
                pl.BlockSpec(source.shape, lambda i, *_: (0, 0, 0)),
            ],
            out_specs=pl.BlockSpec((out_blocks, size, width), lambda i, *_: (0, 0, 0)),
            scratch_shapes=[pltpu.VMEM((out_blocks + 1, size, width), jnp.float32)],
        ),
        out_shape=jax.ShapeDtypeStruct((out_blocks, size, width), out_dtype),
        compiler_params=pltpu.CompilerParams(dimension_semantics=("arbitrary",)),
    )(dest, source_of, count, values, source)


class Group:
    def __init__(self, axis):
        self.axis = axis
        self.n = lax.axis_size(axis)
        self.inner = INNER[axis]
        self.outer = self.n // self.inner
        self.me = lax.axis_index(axis)
        self.o = self.me // self.inner
        self.i = lax.rem(self.me, self.inner)
        self.row, self.col = lax.axis_index("row"), lax.axis_index("col")

    def device(self, peer):
        return (self.row, peer) if self.axis == "col" else (peer, self.col)

    def others_outer(self, k):
        half = k // 2 + 1
        return lax.rem(self.o + jnp.where(k % 2 == 0, half, self.outer - half), self.outer)

    def others_inner(self):
        return [lax.rem(self.i + d, self.inner) for d in range(1, self.inner)]

    def partner(self, k):
        half = k // 2 + 1
        return lax.rem(self.me + jnp.where(k % 2 == 0, half, self.n - half), self.n)

    def copy(self, src, dst, send, recv, peer):
        return pltpu.make_async_remote_copy(
            src_ref=src, dst_ref=dst, send_sem=send, recv_sem=recv,
            device_id=self.device(peer), device_id_type=MESH,
        )

    def hello(self, every):
        barrier = pltpu.get_barrier_semaphore()

        def greet(peer):
            pl.semaphore_signal(barrier, inc=1, device_id=self.device(peer), device_id_type=MESH)

        if every:

            @pl.loop(0, self.n - 1)
            def _(k):
                greet(self.partner(k))

            return self.n - 1

        @pl.loop(0, self.outer - 1)
        def _(k):
            greet(self.others_outer(k) * self.inner + self.i)

        for i in self.others_inner():
            greet(self.o * self.inner + i)
        return self.outer - 1 + self.inner - 1


class Gather:
    def __init__(self, group, src, held, send, recv):
        self.g, self.src, self.held, self.send, self.recv = group, src, held, send, recv

    def to_outer(self, o):
        g = self.g
        peer = o * g.inner + g.i
        return g.copy(self.src, self.held.at[g.me], self.send.at[peer], self.recv.at[g.me], peer)

    def from_slot(self, slot, peer):
        return self.g.copy(self.src, self.held.at[slot], self.send.at[slot], self.recv.at[slot], peer)

    def forward(self, o, i):
        g = self.g
        slot = o * g.inner + g.i
        return g.copy(self.held.at[slot], self.held.at[slot], self.send.at[o * g.inner + i],
                      self.recv.at[slot], g.o * g.inner + i)

    def own_inner(self, i):
        g = self.g
        peer = g.o * g.inner + i
        return g.copy(self.src, self.held.at[g.me], self.send.at[peer], self.recv.at[g.me], peer)

    def start(self):
        g = self.g

        @pl.loop(0, g.outer - 1)
        def _(k):
            self.to_outer(g.others_outer(k)).start()

        for i in self.near():
            self.own_inner(i).start()

    def near(self):
        g = self.g
        if g.inner == 4:
            return [lax.rem(g.i + 1, 4), lax.rem(g.i + 3, 4)]
        return g.others_inner()

    def second(self, o):
        g = self.g
        even = lax.rem(o, 2) == 0
        source = lax.rem(g.i + jnp.where(even, 3, 1), 4)
        target = lax.rem(g.i + jnp.where(even, 1, 3), 4)
        opposite = lax.rem(g.i + 2, 4)
        slot = o * g.inner + source
        return g.copy(self.held.at[slot], self.held.at[slot], self.send.at[o * g.inner + opposite],
                      self.recv.at[slot], g.o * g.inner + target), source, target

    def pass_on(self, o):
        g = self.g
        if g.inner == 4:
            copy, source, _ = self.second(o)
            self.from_slot(o * g.inner + source, g.o * g.inner + source).wait_recv()
            copy.start()

    def remaining(self, o):
        g = self.g
        if g.inner == 4:
            return [self.second(o)[2], lax.rem(g.i + 2, 4)]
        return g.others_inner()

    def relay(self):
        g = self.g

        @pl.loop(0, g.outer - 1)
        def _(k):
            o = g.others_outer(k)
            slot = o * g.inner + g.i
            self.from_slot(slot, slot).wait_recv()
            for i in self.near():
                self.forward(o, i).start()
            self.pass_on(jnp.where(k == 0, g.o, g.others_outer(jnp.maximum(k - 1, 0))))

        self.pass_on(g.others_outer(g.outer - 2) if g.outer > 1 else g.o)

    def finish(self):
        g = self.g
        for i in self.remaining(g.o):
            peer = g.o * g.inner + i
            self.from_slot(peer, peer).wait_recv()

        @pl.loop(0, g.outer - 1)
        def _(k):
            o = g.others_outer(k)
            for i in self.remaining(o):
                slot = o * g.inner + i
                self.from_slot(slot, g.o * g.inner + i).wait_recv()

    def drain(self):
        g = self.g

        @pl.loop(0, g.outer - 1)
        def _(k):
            o = g.others_outer(k)
            self.to_outer(o).wait_send()
            for i in self.near():
                self.forward(o, i).wait_send()
            if g.inner == 4:
                self.second(o)[0].wait_send()

        for i in self.near():
            self.own_inner(i).wait_send()
        if g.inner == 4:
            self.second(g.o)[0].wait_send()


class Scatter:
    def __init__(self, group, src, near, sums, far, send1, recv1, send2, recv2):
        self.g, self.src, self.near, self.sums, self.far = group, src, near, sums, far
        self.send1, self.recv1, self.send2, self.recv2 = send1, recv1, send2, recv2

    def along_inner(self, o, i):
        g = self.g
        slot = o * g.inner + i
        return g.copy(self.src.at[slot], self.near.at[o * g.inner + g.i], self.send1.at[slot],
                      self.recv1.at[o * g.inner + g.i], g.o * g.inner + i)

    def arrived_inner(self, o, i):
        g = self.g
        slot = o * g.inner + i
        return g.copy(self.src.at[slot], self.near.at[slot], self.send1.at[slot], self.recv1.at[slot],
                      g.o * g.inner + i)

    def along_outer(self, o):
        g = self.g
        return g.copy(self.sums.at[o], self.far.at[g.o], self.send2.at[o], self.recv2.at[g.o], o * g.inner + g.i)

    def arrived_outer(self, o):
        g = self.g
        return g.copy(self.sums.at[o], self.far.at[o], self.send2.at[o], self.recv2.at[o], o * g.inner + g.i)

    def start(self):
        g = self.g

        @pl.loop(0, g.outer - 1)
        def _(k):
            for i in g.others_inner():
                self.along_inner(g.others_outer(k), i).start()

        for i in g.others_inner():
            self.along_inner(g.o, i).start()

    def near_sum(self, o):
        g = self.g
        for i in g.others_inner():
            self.arrived_inner(o, i).wait_recv()
        total = self.src[o * g.inner + g.i].astype(jnp.float32)
        for i in g.others_inner():
            total += self.near[o * g.inner + i].astype(jnp.float32)
        return total

    def relay(self):
        g = self.g

        @pl.loop(0, g.outer - 1)
        def _(k):
            o = g.others_outer(k)
            self.sums[o] = self.near_sum(o)
            self.along_outer(o).start()

    def finish(self):
        g = self.g
        own = self.near_sum(g.o)

        def add(k, total):
            o = g.others_outer(k)
            self.arrived_outer(o).wait_recv()
            return total + self.far[o]

        return lax.fori_loop(0, g.outer - 1, add, own)

    def drain(self):
        g = self.g

        @pl.loop(0, g.outer - 1)
        def _(k):
            o = g.others_outer(k)
            self.along_outer(o).wait_send()
            for i in g.others_inner():
                self.along_inner(o, i).wait_send()

        for i in g.others_inner():
            self.along_inner(g.o, i).wait_send()


def gather_kernel(axis, src, out, held, send, recv):
    g = Group(axis)
    gather = Gather(g, src, held, send, recv)
    pl.semaphore_wait(pltpu.get_barrier_semaphore(), g.hello(False))
    gather.start()
    held[g.me] = src[...]
    gather.relay()
    gather.finish()
    out[...] = held[...]
    gather.drain()


def middle_kernel(
    per_slice, norm_factor, part, weight, bias, cotangent,
    hidden_out, out, slice_out,
    near, sums, far, send1, recv1, send2, recv2,
    own, slices, held, send, recv,
    near_b, sums_b, far_b, send1_b, recv1_b, send2_b, recv2_b,
):
    g = Group("col")
    scatter = Scatter(g, part, near, sums, far, send1, recv1, send2, recv2)
    gather = Gather(g, own, held, send, recv)
    small = Scatter(g, slices, near_b, sums_b, far_b, send1_b, recv1_b, send2_b, recv2_b)
    pl.semaphore_wait(pltpu.get_barrier_semaphore(), g.hello(False))
    scatter.start()
    scatter.relay()
    aggregated = scatter.finish()

    highest = lax.Precision.HIGHEST
    pre_act = jnp.dot(aggregated, weight[...], precision=highest, preferred_element_type=jnp.float32) + bias[...]
    sigm = 1.0 / (1.0 + jnp.exp(-pre_act))
    masked_grad = cotangent[...].astype(jnp.float32) * sigm * (1.0 + pre_act * (1.0 - sigm))
    grad_t = lax.dot_general(
        weight[...], masked_grad, (((1,), (1,)), ((), ())), precision=highest, preferred_element_type=jnp.float32
    ).astype(own.dtype)
    own[...] = grad_t
    held[g.me] = grad_t
    hidden_out[...] = pre_act * sigm
    bias_part = jnp.sum(masked_grad, axis=0, keepdims=True) * norm_factor
    gather.start()
    weight_part = norm_factor * lax.dot_general(
        aggregated, masked_grad, (((0,), (0,)), ((), ())), precision=highest, preferred_element_type=jnp.float32
    )
    spare = slices.shape[1] - per_slice
    for s in range(g.n):
        slices[s, 0:per_slice] = weight_part[s * per_slice : (s + 1) * per_slice]
        slices[s, per_slice:] = jnp.broadcast_to(bias_part, (spare, bias_part.shape[1]))
    gather.relay()
    small.start()
    small.relay()
    slice_out[...] = small.finish()
    gather.finish()
    out[...] = held[...]
    scatter.drain()
    gather.drain()
    small.drain()


def output_kernel(per_slice, hidden, grad_t, slices, hidden_out, grad_out, weight_out, bias_out):
    hidden_out[...] = hidden[...]
    grad_out[...] = grad_t[...].T
    for s in range(slices.shape[0]):
        weight_out[s * per_slice : (s + 1) * per_slice] = slices[s, 0:per_slice]
    bias_out[...] = slices[0, per_slice : per_slice + 1]


def last_kernel(back, part, out, all_out, held, held_part, own, held_all, sb, rb, sp, rp, sa, ra):
    g, c = Group("row"), Group("col")
    gather = Gather(c, own, held_all, sa, ra)

    def block(peer, slot):
        return g.copy(back.at[peer], held.at[slot], sb.at[peer], rb.at[slot], peer)

    def piece(peer, slot):
        return g.copy(part, held_part.at[slot], sp.at[peer], rp.at[slot], peer)

    pl.semaphore_wait(pltpu.get_barrier_semaphore(), g.hello(True) + c.hello(False))

    @pl.loop(0, g.n - 1)
    def _(k):
        piece(g.partner(k), g.me).start()

    @pl.loop(0, g.n - 1)
    def _(k):
        block(g.partner(k), g.me).start()

    held_part[g.me] = part[...]

    @pl.loop(0, g.n - 1)
    def _(k):
        piece(g.partner(k), g.partner(k)).wait_recv()

    total = held_part[0]
    for s in range(1, g.n):
        total += held_part[s]
    own[...] = total
    held_all[c.me] = total
    gather.start()

    def add(k, total):
        block(g.partner(k), g.partner(k)).wait_recv()
        return total + held[g.partner(k)].astype(jnp.float32)

    gather.relay()
    out[...] = lax.fori_loop(0, g.n - 1, add, back[g.me].astype(jnp.float32))
    gather.finish()
    all_out[...] = held_all[...]
    gather.drain()

    @pl.loop(0, g.n - 1)
    def _(k):
        block(g.partner(k), g.partner(k)).wait_send()
        piece(g.partner(k), g.partner(k)).wait_send()


def call(kernel, number, outs, scratch, *arrays):
    vmem = pl.BlockSpec(memory_space=pltpu.VMEM)
    return pl.pallas_call(
        kernel,
        out_shape=outs,
        in_specs=[vmem] * len(arrays),
        out_specs=[vmem] * len(outs),
        scratch_shapes=scratch,
        compiler_params=pltpu.CompilerParams(collective_id=number, has_side_effects=True),
    )(*arrays)


def copies(*sizes):
    return [pltpu.SemaphoreType.DMA((size,)) for size in sizes]


def gather_scratch(n, block, dtype):
    return [pltpu.VMEM((n,) + block, dtype)] + copies(n, n)


def scatter_scratch(axis, block, dtype):
    n = lax.axis_size(axis)
    outer = n // INNER[axis]
    return [
        pltpu.VMEM((n,) + block, dtype),
        pltpu.VMEM((outer,) + block, jnp.float32),
        pltpu.VMEM((outer,) + block, jnp.float32),
    ] + copies(n, n, outer, outer)


def per_device(features, block_values, block_rows, block_cols, counts, weight, bias, cotangent):
    size, width = features.shape
    hidden_width = weight.shape[1]
    row_count = lax.axis_size("row")
    col_count = lax.axis_size("col")
    values = block_values[0, 0]
    rows = block_rows[0, 0]
    cols = block_cols[0, 0]
    count = counts[0]

    shape = jax.ShapeDtypeStruct
    block = (size, width)
    (column_feats,) = call(
        functools.partial(gather_kernel, "row"), 0, [shape((row_count,) + block, features.dtype)],
        gather_scratch(row_count, block, features.dtype), features,
    )
    partial = tile_product(values, rows, cols, count, column_feats, col_count, False, jnp.bfloat16)
    norm_factor = 1.0 / math.sqrt(size * row_count * col_count)
    per_slice = width // col_count
    piece = (per_slice + 1 + -(per_slice + 1) % 8, hidden_width)
    hidden, grad_row, col_slice = call(
        functools.partial(middle_kernel, per_slice, norm_factor), 2,
        [
            shape((size, hidden_width), jnp.float32),
            shape((col_count, width, size), jnp.bfloat16),
            shape(piece, jnp.float32),
        ],
        scatter_scratch("col", block, partial.dtype)
        + [pltpu.VMEM((width, size), jnp.bfloat16), pltpu.VMEM((col_count,) + piece, jnp.float32)]
        + gather_scratch(col_count, (width, size), jnp.bfloat16)
        + scatter_scratch("col", piece, jnp.float32),
        partial, weight, bias[None, :], cotangent,
    )
    back = tile_product(values, cols, rows, count, grad_row, row_count, True, jnp.bfloat16)
    grad_t, all_slices = call(
        last_kernel, 3, [shape(back.shape[1:], jnp.float32), shape((col_count,) + piece, jnp.float32)],
        [
            pltpu.VMEM(back.shape, back.dtype),
            pltpu.VMEM((row_count,) + piece, jnp.float32),
            pltpu.VMEM(piece, jnp.float32),
            pltpu.VMEM((col_count,) + piece, jnp.float32),
        ]
        + copies(row_count, row_count, row_count, row_count, col_count, col_count),
        back, col_slice,
    )
    vmem = pl.BlockSpec(memory_space=pltpu.VMEM)
    hidden, grad_features, grad_weight, grad_bias = pl.pallas_call(
        functools.partial(output_kernel, per_slice),
        out_shape=[
            shape(hidden.shape, jnp.float32),
            shape(block, jnp.float32),
            shape((width, hidden_width), jnp.float32),
            shape((1, hidden_width), jnp.float32),
        ],
        in_specs=[vmem] * 3,
        out_specs=[vmem] * 4,
    )(hidden, grad_t, all_slices)
    return (hidden, grad_features, grad_weight, grad_bias[0])


def solution(mesh):
    placed = (
        P(("row", "col"), None),
        P("row", "col", None, None, None),
        P("row", "col", None),
        P("row", "col", None),
        P("row", "col"),
        P(),
        P(),
        P(("row", "col"), None),
    )
    return jax.shard_map(
        per_device,
        mesh=mesh,
        in_specs=placed,
        out_specs=(P(("row", "col"), None), P(("row", "col"), None), P(), P()),
        check_vma=False,
    )
```

```python
import functools
import math

import jax
import jax.numpy as jnp
from jax import lax
from jax.experimental import pallas as pl
from jax.experimental.pallas import tpu as pltpu
from jax.sharding import PartitionSpec as P

MESH = pl.DeviceIdType.MESH
CHUNK = 16
INNER = {"row": 2, "col": 4}


def product_kernel(transposed, out_blocks, dest_ref, from_ref, count_ref, values_ref, source_ref, out_ref, totals):
    step = pl.program_id(0)
    live = count_ref[0]

    @pl.when(step == 0)
    def _():
        totals[...] = jnp.zeros_like(totals)

    @pl.when(step * CHUNK < live)
    def _():
        for k in range(CHUNK):
            slot = step * CHUNK + k
            dest = jnp.where(slot < live, dest_ref[slot], out_blocks)
            block = values_ref[k]
            source = source_ref[from_ref[slot]]
            if transposed:
                part = jnp.dot(source, block, preferred_element_type=jnp.float32)
            else:
                part = jnp.dot(block, source, preferred_element_type=jnp.float32)
            totals[dest] += part

    @pl.when(step == pl.num_programs(0) - 1)
    def _():
        out_ref[...] = totals[0:out_blocks].astype(out_ref.dtype)


def tile_product(values, dest, source_of, count, source, out_blocks, transposed, out_dtype):
    slots, size, _ = values.shape
    width = source.shape[2]
    return pl.pallas_call(
        functools.partial(product_kernel, transposed, out_blocks),
        grid_spec=pltpu.PrefetchScalarGridSpec(
            num_scalar_prefetch=3,
            grid=(slots // CHUNK,),
            in_specs=[
                pl.BlockSpec((CHUNK, size, size), lambda i, *_: (i, 0, 0)),
                pl.BlockSpec(source.shape, lambda i, *_: (0, 0, 0)),
            ],
            out_specs=pl.BlockSpec((out_blocks, size, width), lambda i, *_: (0, 0, 0)),
            scratch_shapes=[pltpu.VMEM((out_blocks + 1, size, width), jnp.float32)],
        ),
        out_shape=jax.ShapeDtypeStruct((out_blocks, size, width), out_dtype),
        compiler_params=pltpu.CompilerParams(dimension_semantics=("arbitrary",)),
    )(dest, source_of, count, values, source)


class Group:
    def __init__(self, axis):
        self.axis = axis
        self.n = lax.axis_size(axis)
        self.inner = INNER[axis]
        self.outer = self.n // self.inner
        self.me = lax.axis_index(axis)
        self.o = self.me // self.inner
        self.i = lax.rem(self.me, self.inner)
        self.row, self.col = lax.axis_index("row"), lax.axis_index("col")

    def device(self, peer):
        return (self.row, peer) if self.axis == "col" else (peer, self.col)

    def others_outer(self, k):
        half = k // 2 + 1
        return lax.rem(self.o + jnp.where(k % 2 == 0, half, self.outer - half), self.outer)

    def others_inner(self):
        return [lax.rem(self.i + d, self.inner) for d in range(1, self.inner)]

    def partner(self, k):
        half = k // 2 + 1
        return lax.rem(self.me + jnp.where(k % 2 == 0, half, self.n - half), self.n)

    def copy(self, src, dst, send, recv, peer):
        return pltpu.make_async_remote_copy(
            src_ref=src, dst_ref=dst, send_sem=send, recv_sem=recv,
            device_id=self.device(peer), device_id_type=MESH,
        )

    def hello(self, every):
        barrier = pltpu.get_barrier_semaphore()

        def greet(peer):
            pl.semaphore_signal(barrier, inc=1, device_id=self.device(peer), device_id_type=MESH)

        if every:

            @pl.loop(0, self.n - 1)
            def _(k):
                greet(self.partner(k))

            return self.n - 1

        @pl.loop(0, self.outer - 1)
        def _(k):
            greet(self.others_outer(k) * self.inner + self.i)

        for i in self.others_inner():
            greet(self.o * self.inner + i)
        return self.outer - 1 + self.inner - 1


class Gather:
    def __init__(self, group, src, held, send, recv):
        self.g, self.src, self.held, self.send, self.recv = group, src, held, send, recv

    def to_outer(self, o):
        g = self.g
        peer = o * g.inner + g.i
        return g.copy(self.src, self.held.at[g.me], self.send.at[peer], self.recv.at[g.me], peer)

    def from_slot(self, slot, peer):
        return self.g.copy(self.src, self.held.at[slot], self.send.at[slot], self.recv.at[slot], peer)

    def forward(self, o, i):
        g = self.g
        slot = o * g.inner + g.i
        return g.copy(self.held.at[slot], self.held.at[slot], self.send.at[o * g.inner + i],
                      self.recv.at[slot], g.o * g.inner + i)

    def own_inner(self, i):
        g = self.g
        peer = g.o * g.inner + i
        return g.copy(self.src, self.held.at[g.me], self.send.at[peer], self.recv.at[g.me], peer)

    def start(self):
        g = self.g

        @pl.loop(0, g.outer - 1)
        def _(k):
            self.to_outer(g.others_outer(k)).start()

        for i in g.others_inner():
            self.own_inner(i).start()

    def relay(self):
        g = self.g

        @pl.loop(0, g.outer - 1)
        def _(k):
            o = g.others_outer(k)
            slot = o * g.inner + g.i
            self.from_slot(slot, slot).wait_recv()
            for i in g.others_inner():
                self.forward(o, i).start()

    def finish(self):
        g = self.g
        for i in g.others_inner():
            peer = g.o * g.inner + i
            self.from_slot(peer, peer).wait_recv()

        @pl.loop(0, g.outer - 1)
        def _(k):
            o = g.others_outer(k)
            for i in g.others_inner():
                slot = o * g.inner + i
                self.from_slot(slot, g.o * g.inner + i).wait_recv()

    def drain(self):
        g = self.g

        @pl.loop(0, g.outer - 1)
        def _(k):
            o = g.others_outer(k)
            self.to_outer(o).wait_send()
            for i in g.others_inner():
                self.forward(o, i).wait_send()

        for i in g.others_inner():
            self.own_inner(i).wait_send()


class Scatter:
    def __init__(self, group, src, near, sums, far, send1, recv1, send2, recv2):
        self.g, self.src, self.near, self.sums, self.far = group, src, near, sums, far
        self.send1, self.recv1, self.send2, self.recv2 = send1, recv1, send2, recv2

    def along_inner(self, o, i):
        g = self.g
        slot = o * g.inner + i
        return g.copy(self.src.at[slot], self.near.at[o * g.inner + g.i], self.send1.at[slot],
                      self.recv1.at[o * g.inner + g.i], g.o * g.inner + i)

    def arrived_inner(self, o, i):
        g = self.g
        slot = o * g.inner + i
        return g.copy(self.src.at[slot], self.near.at[slot], self.send1.at[slot], self.recv1.at[slot],
                      g.o * g.inner + i)

    def along_outer(self, o):
        g = self.g
        return g.copy(self.sums.at[o], self.far.at[g.o], self.send2.at[o], self.recv2.at[g.o], o * g.inner + g.i)

    def arrived_outer(self, o):
        g = self.g
        return g.copy(self.sums.at[o], self.far.at[o], self.send2.at[o], self.recv2.at[o], o * g.inner + g.i)

    def start(self):
        g = self.g

        @pl.loop(0, g.outer - 1)
        def _(k):
            for i in g.others_inner():
                self.along_inner(g.others_outer(k), i).start()

        for i in g.others_inner():
            self.along_inner(g.o, i).start()

    def near_sum(self, o):
        g = self.g
        for i in g.others_inner():
            self.arrived_inner(o, i).wait_recv()
        total = self.src[o * g.inner + g.i].astype(jnp.float32)
        for i in g.others_inner():
            total += self.near[o * g.inner + i].astype(jnp.float32)
        return total

    def relay(self):
        g = self.g

        @pl.loop(0, g.outer - 1)
        def _(k):
            o = g.others_outer(k)
            self.sums[o] = self.near_sum(o)
            self.along_outer(o).start()

    def finish(self):
        g = self.g
        own = self.near_sum(g.o)

        def add(k, total):
            o = g.others_outer(k)
            self.arrived_outer(o).wait_recv()
            return total + self.far[o]

        return lax.fori_loop(0, g.outer - 1, add, own)

    def drain(self):
        g = self.g

        @pl.loop(0, g.outer - 1)
        def _(k):
            o = g.others_outer(k)
            self.along_outer(o).wait_send()
            for i in g.others_inner():
                self.along_inner(o, i).wait_send()

        for i in g.others_inner():
            self.along_inner(g.o, i).wait_send()


def gather_kernel(axis, src, out, held, send, recv):
    g = Group(axis)
    gather = Gather(g, src, held, send, recv)
    pl.semaphore_wait(pltpu.get_barrier_semaphore(), g.hello(False))
    gather.start()
    held[g.me] = src[...]
    gather.relay()
    gather.finish()
    out[...] = held[...]
    gather.drain()


def middle_kernel(
    per_slice, norm_factor, part, weight, bias, cotangent,
    hidden_out, out, slice_out,
    near, sums, far, send1, recv1, send2, recv2,
    own, slices, held, send, recv,
    near_b, sums_b, far_b, send1_b, recv1_b, send2_b, recv2_b,
):
    g = Group("col")
    scatter = Scatter(g, part, near, sums, far, send1, recv1, send2, recv2)
    gather = Gather(g, own, held, send, recv)
    small = Scatter(g, slices, near_b, sums_b, far_b, send1_b, recv1_b, send2_b, recv2_b)
    pl.semaphore_wait(pltpu.get_barrier_semaphore(), g.hello(False))
    scatter.start()
    scatter.relay()
    aggregated = scatter.finish()

    highest = lax.Precision.HIGHEST
    pre_act = jnp.dot(aggregated, weight[...], precision=highest, preferred_element_type=jnp.float32) + bias[...]
    sigm = 1.0 / (1.0 + jnp.exp(-pre_act))
    masked_grad = cotangent[...].astype(jnp.float32) * sigm * (1.0 + pre_act * (1.0 - sigm))
    grad_t = lax.dot_general(
        weight[...], masked_grad, (((1,), (1,)), ((), ())), precision=highest, preferred_element_type=jnp.float32
    ).astype(own.dtype)
    own[...] = grad_t
    held[g.me] = grad_t
    hidden_out[...] = pre_act * sigm
    bias_part = jnp.sum(masked_grad, axis=0, keepdims=True) * norm_factor
    gather.start()
    weight_part = norm_factor * lax.dot_general(
        aggregated, masked_grad, (((0,), (0,)), ((), ())), precision=highest, preferred_element_type=jnp.float32
    )
    spare = slices.shape[1] - per_slice
    for s in range(g.n):
        slices[s, 0:per_slice] = weight_part[s * per_slice : (s + 1) * per_slice]
        slices[s, per_slice:] = jnp.broadcast_to(bias_part, (spare, bias_part.shape[1]))
    small.start()
    gather.relay()
    small.relay()
    gather.finish()
    out[...] = held[...]
    slice_out[...] = small.finish()
    scatter.drain()
    gather.drain()
    small.drain()


def output_kernel(per_slice, hidden, grad_t, slices, hidden_out, grad_out, weight_out, bias_out):
    hidden_out[...] = hidden[...]
    grad_out[...] = grad_t[...].T
    for s in range(slices.shape[0]):
        weight_out[s * per_slice : (s + 1) * per_slice] = slices[s, 0:per_slice]
    bias_out[...] = slices[0, per_slice : per_slice + 1]


def last_kernel(back, part, out, all_out, held, held_part, own, held_all, sb, rb, sp, rp, sa, ra):
    g, c = Group("row"), Group("col")
    gather = Gather(c, own, held_all, sa, ra)

    def block(peer, slot):
        return g.copy(back.at[peer], held.at[slot], sb.at[peer], rb.at[slot], peer)

    def piece(peer, slot):
        return g.copy(part, held_part.at[slot], sp.at[peer], rp.at[slot], peer)

    pl.semaphore_wait(pltpu.get_barrier_semaphore(), g.hello(True) + c.hello(False))

    @pl.loop(0, g.n - 1)
    def _(k):
        piece(g.partner(k), g.me).start()

    @pl.loop(0, g.n - 1)
    def _(k):
        block(g.partner(k), g.me).start()

    held_part[g.me] = part[...]

    @pl.loop(0, g.n - 1)
    def _(k):
        piece(g.partner(k), g.partner(k)).wait_recv()

    total = held_part[0]
    for s in range(1, g.n):
        total += held_part[s]
    own[...] = total
    held_all[c.me] = total
    gather.start()

    def add(k, total):
        block(g.partner(k), g.partner(k)).wait_recv()
        return total + held[g.partner(k)].astype(jnp.float32)

    gather.relay()
    out[...] = lax.fori_loop(0, g.n - 1, add, back[g.me].astype(jnp.float32))
    gather.finish()
    all_out[...] = held_all[...]
    gather.drain()

    @pl.loop(0, g.n - 1)
    def _(k):
        block(g.partner(k), g.partner(k)).wait_send()
        piece(g.partner(k), g.partner(k)).wait_send()


def call(kernel, number, outs, scratch, *arrays):
    vmem = pl.BlockSpec(memory_space=pltpu.VMEM)
    return pl.pallas_call(
        kernel,
        out_shape=outs,
        in_specs=[vmem] * len(arrays),
        out_specs=[vmem] * len(outs),
        scratch_shapes=scratch,
        compiler_params=pltpu.CompilerParams(collective_id=number, has_side_effects=True),
    )(*arrays)


def copies(*sizes):
    return [pltpu.SemaphoreType.DMA((size,)) for size in sizes]


def gather_scratch(n, block, dtype):
    return [pltpu.VMEM((n,) + block, dtype)] + copies(n, n)


def scatter_scratch(axis, block, dtype):
    n = lax.axis_size(axis)
    outer = n // INNER[axis]
    return [
        pltpu.VMEM((n,) + block, dtype),
        pltpu.VMEM((outer,) + block, jnp.float32),
        pltpu.VMEM((outer,) + block, jnp.float32),
    ] + copies(n, n, outer, outer)


def per_device(features, block_values, block_rows, block_cols, counts, weight, bias, cotangent):
    size, width = features.shape
    hidden_width = weight.shape[1]
    row_count = lax.axis_size("row")
    col_count = lax.axis_size("col")
    values = block_values[0, 0]
    rows = block_rows[0, 0]
    cols = block_cols[0, 0]
    count = counts[0]

    shape = jax.ShapeDtypeStruct
    block = (size, width)
    (column_feats,) = call(
        functools.partial(gather_kernel, "row"), 0, [shape((row_count,) + block, features.dtype)],
        gather_scratch(row_count, block, features.dtype), features,
    )
    partial = tile_product(values, rows, cols, count, column_feats, col_count, False, jnp.bfloat16)
    norm_factor = 1.0 / math.sqrt(size * row_count * col_count)
    per_slice = width // col_count
    piece = (per_slice + 1 + -(per_slice + 1) % 8, hidden_width)
    hidden, grad_row, col_slice = call(
        functools.partial(middle_kernel, per_slice, norm_factor), 2,
        [
            shape((size, hidden_width), jnp.float32),
            shape((col_count, width, size), jnp.bfloat16),
            shape(piece, jnp.float32),
        ],
        scatter_scratch("col", block, partial.dtype)
        + [pltpu.VMEM((width, size), jnp.bfloat16), pltpu.VMEM((col_count,) + piece, jnp.float32)]
        + gather_scratch(col_count, (width, size), jnp.bfloat16)
        + scatter_scratch("col", piece, jnp.float32),
        partial, weight, bias[None, :], cotangent,
    )
    back = tile_product(values, cols, rows, count, grad_row, row_count, True, jnp.bfloat16)
    grad_t, all_slices = call(
        last_kernel, 3, [shape(back.shape[1:], jnp.float32), shape((col_count,) + piece, jnp.float32)],
        [
            pltpu.VMEM(back.shape, back.dtype),
            pltpu.VMEM((row_count,) + piece, jnp.float32),
            pltpu.VMEM(piece, jnp.float32),
            pltpu.VMEM((col_count,) + piece, jnp.float32),
        ]
        + copies(row_count, row_count, row_count, row_count, col_count, col_count),
        back, col_slice,
    )
    vmem = pl.BlockSpec(memory_space=pltpu.VMEM)
    hidden, grad_features, grad_weight, grad_bias = pl.pallas_call(
        functools.partial(output_kernel, per_slice),
        out_shape=[
            shape(hidden.shape, jnp.float32),
            shape(block, jnp.float32),
            shape((width, hidden_width), jnp.float32),
            shape((1, hidden_width), jnp.float32),
        ],
        in_specs=[vmem] * 3,
        out_specs=[vmem] * 4,
    )(hidden, grad_t, all_slices)
    return (hidden, grad_features, grad_weight, grad_bias[0])


def solution(mesh):
    placed = (
        P(("row", "col"), None),
        P("row", "col", None, None, None),
        P("row", "col", None),
        P("row", "col", None),
        P("row", "col"),
        P(),
        P(),
        P(("row", "col"), None),
    )
    return jax.shard_map(
        per_device,
        mesh=mesh,
        in_specs=placed,
        out_specs=(P(("row", "col"), None), P(("row", "col"), None), P(), P()),
        check_vma=False,
    )
```

```python
import functools
import math

import jax
import jax.numpy as jnp
from jax import lax
from jax.experimental import pallas as pl
from jax.experimental.pallas import tpu as pltpu
from jax.sharding import PartitionSpec as P

MESH = pl.DeviceIdType.MESH
CHUNK = 16
INNER = {"row": 2, "col": 4}


def product_kernel(transposed, out_blocks, dest_ref, from_ref, count_ref, values_ref, source_ref, out_ref, totals):
    step = pl.program_id(0)
    live = count_ref[0]

    @pl.when(step == 0)
    def _():
        totals[...] = jnp.zeros_like(totals)

    @pl.when(step * CHUNK < live)
    def _():
        for k in range(CHUNK):
            slot = step * CHUNK + k
            dest = jnp.where(slot < live, dest_ref[slot], out_blocks)
            block = values_ref[k]
            source = source_ref[from_ref[slot]]
            if transposed:
                part = jnp.dot(source, block, preferred_element_type=jnp.float32)
            else:
                part = jnp.dot(block, source, preferred_element_type=jnp.float32)
            totals[dest] += part

    @pl.when(step == pl.num_programs(0) - 1)
    def _():
        out_ref[...] = totals[0:out_blocks].astype(out_ref.dtype)


def tile_product(values, dest, source_of, count, source, out_blocks, transposed, out_dtype):
    slots, size, _ = values.shape
    width = source.shape[2]
    return pl.pallas_call(
        functools.partial(product_kernel, transposed, out_blocks),
        grid_spec=pltpu.PrefetchScalarGridSpec(
            num_scalar_prefetch=3,
            grid=(slots // CHUNK,),
            in_specs=[
                pl.BlockSpec((CHUNK, size, size), lambda i, *_: (i, 0, 0)),
                pl.BlockSpec(source.shape, lambda i, *_: (0, 0, 0)),
            ],
            out_specs=pl.BlockSpec((out_blocks, size, width), lambda i, *_: (0, 0, 0)),
            scratch_shapes=[pltpu.VMEM((out_blocks + 1, size, width), jnp.float32)],
        ),
        out_shape=jax.ShapeDtypeStruct((out_blocks, size, width), out_dtype),
        compiler_params=pltpu.CompilerParams(dimension_semantics=("arbitrary",)),
    )(dest, source_of, count, values, source)


class Group:
    def __init__(self, axis):
        self.axis = axis
        self.n = lax.axis_size(axis)
        self.inner = INNER[axis]
        self.outer = self.n // self.inner
        self.me = lax.axis_index(axis)
        self.o = self.me // self.inner
        self.i = lax.rem(self.me, self.inner)
        self.row, self.col = lax.axis_index("row"), lax.axis_index("col")

    def device(self, peer):
        return (self.row, peer) if self.axis == "col" else (peer, self.col)

    def others_outer(self, k):
        half = k // 2 + 1
        return lax.rem(self.o + jnp.where(k % 2 == 0, half, self.outer - half), self.outer)

    def far_first(self, k):
        return self.others_outer(self.outer - 2 - k)

    def others_inner(self):
        return [lax.rem(self.i + d, self.inner) for d in range(1, self.inner)]

    def partner(self, k):
        half = k // 2 + 1
        return lax.rem(self.me + jnp.where(k % 2 == 0, half, self.n - half), self.n)

    def copy(self, src, dst, send, recv, peer):
        return pltpu.make_async_remote_copy(
            src_ref=src, dst_ref=dst, send_sem=send, recv_sem=recv,
            device_id=self.device(peer), device_id_type=MESH,
        )

    def hello(self, every):
        barrier = pltpu.get_barrier_semaphore()

        def greet(peer):
            pl.semaphore_signal(barrier, inc=1, device_id=self.device(peer), device_id_type=MESH)

        if every:

            @pl.loop(0, self.n - 1)
            def _(k):
                greet(self.partner(k))

            return self.n - 1

        @pl.loop(0, self.outer - 1)
        def _(k):
            greet(self.others_outer(k) * self.inner + self.i)

        for i in self.others_inner():
            greet(self.o * self.inner + i)
        return self.outer - 1 + self.inner - 1


class Gather:
    def __init__(self, group, src, held, send, recv):
        self.g, self.src, self.held, self.send, self.recv = group, src, held, send, recv

    def to_outer(self, o):
        g = self.g
        peer = o * g.inner + g.i
        return g.copy(self.src, self.held.at[g.me], self.send.at[peer], self.recv.at[g.me], peer)

    def from_slot(self, slot, peer):
        return self.g.copy(self.src, self.held.at[slot], self.send.at[slot], self.recv.at[slot], peer)

    def forward(self, o, i):
        g = self.g
        slot = o * g.inner + g.i
        return g.copy(self.held.at[slot], self.held.at[slot], self.send.at[o * g.inner + i],
                      self.recv.at[slot], g.o * g.inner + i)

    def own_inner(self, i):
        g = self.g
        peer = g.o * g.inner + i
        return g.copy(self.src, self.held.at[g.me], self.send.at[peer], self.recv.at[g.me], peer)

    def start(self):
        g = self.g

        @pl.loop(0, g.outer - 1)
        def _(k):
            self.to_outer(g.others_outer(k)).start()

        for i in g.others_inner():
            self.own_inner(i).start()

    def relay(self):
        g = self.g

        @pl.loop(0, g.outer - 1)
        def _(k):
            o = g.others_outer(k)
            slot = o * g.inner + g.i
            self.from_slot(slot, slot).wait_recv()
            for i in g.others_inner():
                self.forward(o, i).start()

    def finish(self):
        g = self.g
        for i in g.others_inner():
            peer = g.o * g.inner + i
            self.from_slot(peer, peer).wait_recv()

        @pl.loop(0, g.outer - 1)
        def _(k):
            o = g.others_outer(k)
            for i in g.others_inner():
                slot = o * g.inner + i
                self.from_slot(slot, g.o * g.inner + i).wait_recv()

    def drain(self):
        g = self.g

        @pl.loop(0, g.outer - 1)
        def _(k):
            o = g.others_outer(k)
            self.to_outer(o).wait_send()
            for i in g.others_inner():
                self.forward(o, i).wait_send()

        for i in g.others_inner():
            self.own_inner(i).wait_send()


class Scatter:
    def __init__(self, group, src, near, sums, far, send1, recv1, send2, recv2):
        self.g, self.src, self.near, self.sums, self.far = group, src, near, sums, far
        self.send1, self.recv1, self.send2, self.recv2 = send1, recv1, send2, recv2

    def along_inner(self, o, i):
        g = self.g
        slot = o * g.inner + i
        return g.copy(self.src.at[slot], self.near.at[o * g.inner + g.i], self.send1.at[slot],
                      self.recv1.at[o * g.inner + g.i], g.o * g.inner + i)

    def arrived_inner(self, o, i):
        g = self.g
        slot = o * g.inner + i
        return g.copy(self.src.at[slot], self.near.at[slot], self.send1.at[slot], self.recv1.at[slot],
                      g.o * g.inner + i)

    def along_outer(self, o):
        g = self.g
        return g.copy(self.sums.at[o], self.far.at[g.o], self.send2.at[o], self.recv2.at[g.o], o * g.inner + g.i)

    def arrived_outer(self, o):
        g = self.g
        return g.copy(self.sums.at[o], self.far.at[o], self.send2.at[o], self.recv2.at[o], o * g.inner + g.i)

    def start(self):
        g = self.g

        @pl.loop(0, g.outer - 1)
        def _(k):
            for i in g.others_inner():
                self.along_inner(g.far_first(k), i).start()

        for i in g.others_inner():
            self.along_inner(g.o, i).start()

    def near_sum(self, o):
        g = self.g
        for i in g.others_inner():
            self.arrived_inner(o, i).wait_recv()
        total = self.src[o * g.inner + g.i].astype(jnp.float32)
        for i in g.others_inner():
            total += self.near[o * g.inner + i].astype(jnp.float32)
        return total

    def relay(self):
        g = self.g

        @pl.loop(0, g.outer - 1)
        def _(k):
            o = g.far_first(k)
            self.sums[o] = self.near_sum(o)
            self.along_outer(o).start()

    def finish(self):
        g = self.g
        own = self.near_sum(g.o)

        def add(k, total):
            o = g.far_first(k)
            self.arrived_outer(o).wait_recv()
            return total + self.far[o]

        return lax.fori_loop(0, g.outer - 1, add, own)

    def drain(self):
        g = self.g

        @pl.loop(0, g.outer - 1)
        def _(k):
            o = g.far_first(k)
            self.along_outer(o).wait_send()
            for i in g.others_inner():
                self.along_inner(o, i).wait_send()

        for i in g.others_inner():
            self.along_inner(g.o, i).wait_send()


def gather_kernel(axis, src, out, held, send, recv):
    g = Group(axis)
    gather = Gather(g, src, held, send, recv)
    pl.semaphore_wait(pltpu.get_barrier_semaphore(), g.hello(False))
    gather.start()
    held[g.me] = src[...]
    gather.relay()
    gather.finish()
    out[...] = held[...]
    gather.drain()


def middle_kernel(
    per_slice, norm_factor, part, weight, bias, cotangent,
    hidden_out, out, slice_out,
    near, sums, far, send1, recv1, send2, recv2,
    own, slices, held, send, recv,
    near_b, sums_b, far_b, send1_b, recv1_b, send2_b, recv2_b,
):
    g = Group("col")
    scatter = Scatter(g, part, near, sums, far, send1, recv1, send2, recv2)
    gather = Gather(g, own, held, send, recv)
    small = Scatter(g, slices, near_b, sums_b, far_b, send1_b, recv1_b, send2_b, recv2_b)
    pl.semaphore_wait(pltpu.get_barrier_semaphore(), g.hello(False))
    scatter.start()
    scatter.relay()
    aggregated = scatter.finish()

    highest = lax.Precision.HIGHEST
    pre_act = jnp.dot(aggregated, weight[...], precision=highest, preferred_element_type=jnp.float32) + bias[...]
    sigm = 1.0 / (1.0 + jnp.exp(-pre_act))
    masked_grad = cotangent[...].astype(jnp.float32) * sigm * (1.0 + pre_act * (1.0 - sigm))
    grad_t = lax.dot_general(
        weight[...], masked_grad, (((1,), (1,)), ((), ())), precision=highest, preferred_element_type=jnp.float32
    ).astype(own.dtype)
    own[...] = grad_t
    held[g.me] = grad_t
    hidden_out[...] = pre_act * sigm
    bias_part = jnp.sum(masked_grad, axis=0, keepdims=True) * norm_factor
    gather.start()
    weight_part = norm_factor * lax.dot_general(
        aggregated, masked_grad, (((0,), (0,)), ((), ())), precision=highest, preferred_element_type=jnp.float32
    )
    spare = slices.shape[1] - per_slice
    for s in range(g.n):
        slices[s, 0:per_slice] = weight_part[s * per_slice : (s + 1) * per_slice]
        slices[s, per_slice:] = jnp.broadcast_to(bias_part, (spare, bias_part.shape[1]))
    small.start()
    gather.relay()
    small.relay()
    gather.finish()
    out[...] = held[...]
    slice_out[...] = small.finish()
    scatter.drain()
    gather.drain()
    small.drain()


def output_kernel(per_slice, hidden, grad_t, slices, hidden_out, grad_out, weight_out, bias_out):
    hidden_out[...] = hidden[...]
    grad_out[...] = grad_t[...].T
    for s in range(slices.shape[0]):
        weight_out[s * per_slice : (s + 1) * per_slice] = slices[s, 0:per_slice]
    bias_out[...] = slices[0, per_slice : per_slice + 1]


def last_kernel(back, part, out, all_out, held, held_part, own, held_all, sb, rb, sp, rp, sa, ra):
    g, c = Group("row"), Group("col")
    gather = Gather(c, own, held_all, sa, ra)

    def block(peer, slot):
        return g.copy(back.at[peer], held.at[slot], sb.at[peer], rb.at[slot], peer)

    def piece(peer, slot):
        return g.copy(part, held_part.at[slot], sp.at[peer], rp.at[slot], peer)

    pl.semaphore_wait(pltpu.get_barrier_semaphore(), g.hello(True) + c.hello(False))

    @pl.loop(0, g.n - 1)
    def _(k):
        piece(g.partner(k), g.me).start()

    @pl.loop(0, g.n - 1)
    def _(k):
        block(g.partner(k), g.me).start()

    held_part[g.me] = part[...]

    @pl.loop(0, g.n - 1)
    def _(k):
        piece(g.partner(k), g.partner(k)).wait_recv()

    total = held_part[0]
    for s in range(1, g.n):
        total += held_part[s]
    own[...] = total
    held_all[c.me] = total
    gather.start()

    def add(k, total):
        block(g.partner(k), g.partner(k)).wait_recv()
        return total + held[g.partner(k)].astype(jnp.float32)

    gather.relay()
    out[...] = lax.fori_loop(0, g.n - 1, add, back[g.me].astype(jnp.float32))
    gather.finish()
    all_out[...] = held_all[...]
    gather.drain()

    @pl.loop(0, g.n - 1)
    def _(k):
        block(g.partner(k), g.partner(k)).wait_send()
        piece(g.partner(k), g.partner(k)).wait_send()


def call(kernel, number, outs, scratch, *arrays):
    vmem = pl.BlockSpec(memory_space=pltpu.VMEM)
    return pl.pallas_call(
        kernel,
        out_shape=outs,
        in_specs=[vmem] * len(arrays),
        out_specs=[vmem] * len(outs),
        scratch_shapes=scratch,
        compiler_params=pltpu.CompilerParams(collective_id=number, has_side_effects=True),
    )(*arrays)


def copies(*sizes):
    return [pltpu.SemaphoreType.DMA((size,)) for size in sizes]


def gather_scratch(n, block, dtype):
    return [pltpu.VMEM((n,) + block, dtype)] + copies(n, n)


def scatter_scratch(axis, block, dtype):
    n = lax.axis_size(axis)
    outer = n // INNER[axis]
    return [
        pltpu.VMEM((n,) + block, dtype),
        pltpu.VMEM((outer,) + block, jnp.float32),
        pltpu.VMEM((outer,) + block, jnp.float32),
    ] + copies(n, n, outer, outer)


def per_device(features, block_values, block_rows, block_cols, counts, weight, bias, cotangent):
    size, width = features.shape
    hidden_width = weight.shape[1]
    row_count = lax.axis_size("row")
    col_count = lax.axis_size("col")
    values = block_values[0, 0]
    rows = block_rows[0, 0]
    cols = block_cols[0, 0]
    count = counts[0]

    shape = jax.ShapeDtypeStruct
    block = (size, width)
    (column_feats,) = call(
        functools.partial(gather_kernel, "row"), 0, [shape((row_count,) + block, features.dtype)],
        gather_scratch(row_count, block, features.dtype), features,
    )
    partial = tile_product(values, rows, cols, count, column_feats, col_count, False, jnp.bfloat16)
    norm_factor = 1.0 / math.sqrt(size * row_count * col_count)
    per_slice = width // col_count
    piece = (per_slice + 1 + -(per_slice + 1) % 8, hidden_width)
    hidden, grad_row, col_slice = call(
        functools.partial(middle_kernel, per_slice, norm_factor), 2,
        [
            shape((size, hidden_width), jnp.float32),
            shape((col_count, width, size), jnp.bfloat16),
            shape(piece, jnp.float32),
        ],
        scatter_scratch("col", block, partial.dtype)
        + [pltpu.VMEM((width, size), jnp.bfloat16), pltpu.VMEM((col_count,) + piece, jnp.float32)]
        + gather_scratch(col_count, (width, size), jnp.bfloat16)
        + scatter_scratch("col", piece, jnp.float32),
        partial, weight, bias[None, :], cotangent,
    )
    back = tile_product(values, cols, rows, count, grad_row, row_count, True, jnp.bfloat16)
    grad_t, all_slices = call(
        last_kernel, 3, [shape(back.shape[1:], jnp.float32), shape((col_count,) + piece, jnp.float32)],
        [
            pltpu.VMEM(back.shape, back.dtype),
            pltpu.VMEM((row_count,) + piece, jnp.float32),
            pltpu.VMEM(piece, jnp.float32),
            pltpu.VMEM((col_count,) + piece, jnp.float32),
        ]
        + copies(row_count, row_count, row_count, row_count, col_count, col_count),
        back, col_slice,
    )
    vmem = pl.BlockSpec(memory_space=pltpu.VMEM)
    hidden, grad_features, grad_weight, grad_bias = pl.pallas_call(
        functools.partial(output_kernel, per_slice),
        out_shape=[
            shape(hidden.shape, jnp.float32),
            shape(block, jnp.float32),
            shape((width, hidden_width), jnp.float32),
            shape((1, hidden_width), jnp.float32),
        ],
        in_specs=[vmem] * 3,
        out_specs=[vmem] * 4,
    )(hidden, grad_t, all_slices)
    return (hidden, grad_features, grad_weight, grad_bias[0])


def solution(mesh):
    placed = (
        P(("row", "col"), None),
        P("row", "col", None, None, None),
        P("row", "col", None),
        P("row", "col", None),
        P("row", "col"),
        P(),
        P(),
        P(("row", "col"), None),
    )
    return jax.shard_map(
        per_device,
        mesh=mesh,
        in_specs=placed,
        out_specs=(P(("row", "col"), None), P(("row", "col"), None), P(), P()),
        check_vma=False,
    )
```
